32 devices in a mesh: pair: 4 (over z), slab: 8 (over y, x, core).
Axes of the slice: x: 2, y: 2, z: 4, core: 2. Of those that a mesh axis runs over, the one named last changes fastest.
Arguments:
- amplitudes: float32 [288, 8, 32, 288], P('slab', None, None, 'pair'), may hold values from -6 to 6
- integrals: float32 [32, 288, 32, 288], P('pair', None, 'slab'), may hold values from -0.0625 to 0.0625
Outputs:
- cycle: float32 [288, 8, 32, 288], P('pair', None, 'slab')
The draws below stay inside these ranges and needn't reach their ends.
All inputs are finite; a program needn't handle non-finite values.
Results may differ from the reference program's by a relative error of at most 0.00007.
Values sent between devices are 32-bit elements; how exact they have to be, the bound alone decides.
A program may use at most 128 MiB of HBM per device.

```python
import jax
import jax.numpy as jnp
from jax import lax

O = 32
V = 288
IW = 8


def shard_levels(rng, shape, shards, least, high):
    level = 1.0
    for position, blocks in shards:
        heights = jax.random.uniform(jax.random.fold_in(jax.random.fold_in(rng, 6), position), (blocks,), jnp.float32, least / len(shards), high / len(shards))
        level = level * jnp.repeat(jnp.exp(heights), shape[position] // blocks).reshape((-1,) + (1,) * (len(shape) - 1 - position))
    return level


def gaussian(rng, dims, scale, most, pieces=(), held_as=jnp.bfloat16):
    loudness = shard_levels(rng, dims, pieces, -0.22, 0.18) if pieces else 1.0
    values = jax.random.normal(rng, dims, jnp.float32) * scale * loudness
    return jnp.minimum(jnp.maximum(values, -most), most).astype(held_as)


def setup_inputs(seed: int = 0) -> dict:
    key_list = jax.random.split(jax.random.key(seed), 3)
    amplitudes = gaussian(key_list[0], (V, IW, O, V), 1.0, 6.0, ((0, 8), (3, 4)), jnp.float32)
    integrals = gaussian(key_list[1], (O, V, O, V), (O * V) ** -0.5, 0.0625, ((0, 4), (2, 8)), jnp.float32)
    return {"amplitudes": amplitudes, "integrals": integrals}


def reference(amplitudes, integrals):
    combined = 2.0 * amplitudes - jnp.transpose(amplitudes, (3, 1, 2, 0))
    left = combined.reshape(V * IW, O * V)
    right = integrals.reshape(O * V, O * V)
    product = jnp.dot(left, right, precision=lax.Precision.HIGHEST, preferred_element_type=jnp.float32)
    return product.reshape(V, IW, O, V)
```

```python
import functools

import jax
import jax.numpy as jnp
from jax import lax
from jax.experimental import pallas as pl
from jax.experimental.pallas import tpu as pltpu
from jax.sharding import PartitionSpec as P

PART = 2


def contract_kernel(sizes, *refs):
    slabs, pairs, rows, part, held, columns = sizes
    block_refs, (high_ref, low_ref, out_ref, rows_ref, left_ref) = refs[:slabs], refs[slabs:]
    me = lax.axis_index("slab")
    virtuals = slabs * rows
    wide = held * columns
    here = pl.program_id(0)
    tiles = rows_ref.shape[1]
    for code, block_ref in enumerate(block_refs):
        owner = pl.ds(pl.multiple_of((me ^ code) * (rows * part), 8), rows * part)
        for pair in range(pairs):
            for tile in range(tiles):
                lanes = min(128, wide - tile * 128)
                rows_ref[pair, tile, owner, pl.ds(0, lanes)] = block_ref[pair, :, pl.ds(tile * 128, lanes)]

    def picked(pair):
        window = pl.ds(here, virtuals, stride=part)
        return jnp.concatenate([rows_ref[pair, tile, window, :] for tile in range(tiles)], axis=1)[:, :wide]

    def mirrored(pair, carry):
        turned = jnp.transpose(picked(pair))
        target = pl.ds(pl.multiple_of(pair * columns, 8), columns)
        for k in range(held):
            for other in range(pairs):
                left_ref[target, pl.ds(other * wide + k * columns, columns)] = turned[
                    k * columns : (k + 1) * columns, other * columns : (other + 1) * columns
                ]
        return carry

    lax.fori_loop(0, pairs, mirrored, 0)
    for pair in range(pairs):
        window = pl.ds(pair * wide, wide)
        left_ref[:, window] = 2.0 * picked(pair) - left_ref[:, window]
    left = left_ref[...]
    left_high = left.astype(jnp.bfloat16)
    left_low = (left - left_high.astype(jnp.float32)).astype(jnp.bfloat16)
    dot = functools.partial(jnp.dot, preferred_element_type=jnp.float32)
    total = dot(left_high, high_ref[...]) + dot(left_high, low_ref[...]) + dot(left_low, high_ref[...])
    for pair in range(pairs):
        out_ref[pair, 0] = total[pair * columns : (pair + 1) * columns, :]


def contract(blocks, high, low, sizes):
    slabs, pairs, rows, part, held, columns = sizes
    virtuals = slabs * rows
    depth, width = high.shape
    whole = lambda shape: pl.BlockSpec(shape, lambda i: (0,) * len(shape), pipeline_mode=pl.Buffered(1))
    return pl.pallas_call(
        functools.partial(contract_kernel, sizes),
        grid=(part,),
        out_shape=jax.ShapeDtypeStruct((pairs, part, columns, width), jnp.float32),
        in_specs=[whole(block.shape) for block in blocks] + [whole(high.shape), whole(low.shape)],
        out_specs=pl.BlockSpec((pairs, 1, columns, width), lambda i: (0, i, 0, 0)),
        scratch_shapes=[
            pltpu.VMEM((pairs, pl.cdiv(held * columns, 128), virtuals * part, 128), jnp.float32),
            pltpu.VMEM((virtuals, depth), jnp.float32),
        ],
        compiler_params=pltpu.CompilerParams(vmem_limit_bytes=56 * 2**20),
        cost_estimate=pl.CostEstimate(
            flops=6 * virtuals * part * depth * width,
            bytes_accessed=4 * (virtuals * part * (depth + width) + depth * width),
            transcendentals=0,
        ),
    )(*blocks, high, low)


def contract_plain(blocks, high, low, sizes):
    slabs, pairs, rows, part, held, columns = sizes
    virtuals = slabs * rows
    order = lax.axis_index("slab") ^ jnp.arange(slabs)
    whole = jnp.stack(blocks)[order].reshape(slabs, pairs, rows, part, held, columns)
    whole = whole.transpose(3, 4, 0, 2, 1, 5).reshape(part, held, virtuals, virtuals)
    left = 2.0 * whole - jnp.swapaxes(whole, 2, 3)
    left = left.reshape(part, held, virtuals, pairs, columns).transpose(0, 2, 3, 1, 4)
    right = high.astype(jnp.float32) + low.astype(jnp.float32)
    total = jnp.dot(
        left.reshape(part * virtuals, -1), right,
        precision=lax.Precision.HIGH, preferred_element_type=jnp.float32,
    )
    return total.reshape(part, pairs, columns, -1).transpose(1, 0, 2, 3)


def gathered(block, slabs, turn):
    bits = [1 << n for n in range(1, slabs.bit_length() - 1)]
    turn = turn % max(len(bits), 1)
    blocks = {0: block}
    for bit in bits[turn:] + bits[:turn] + [1]:
        swaps = [(n, n ^ bit) for n in range(slabs)]
        for code in sorted(blocks):
            blocks[code ^ bit] = lax.ppermute(blocks[code], "slab", swaps)
    return [blocks[code] for code in range(slabs)]


def shards(amplitudes, integrals):
    pairs, slabs = lax.axis_size("pair"), lax.axis_size("slab")
    rows, batch, occupied, columns = amplitudes.shape
    held = occupied // pairs
    part = PART if batch % PART == 0 else 1
    chunks = batch // part
    sizes = (slabs, pairs, rows, part, held, columns)
    run = contract if columns % 8 == 0 and (rows * part) % 8 == 0 else contract_plain
    right = integrals.reshape(held, pairs, columns, -1).transpose(1, 0, 2, 3)
    right = right.reshape(held * pairs * columns, -1)
    rounded = lax.reduce_precision(right, 8, 7)
    high = rounded.astype(jnp.bfloat16)
    low = (right - rounded).astype(jnp.bfloat16)
    regrouped = []
    for chunk in range(chunks):
        block = lax.slice_in_dim(amplitudes, chunk * part, (chunk + 1) * part, axis=1)
        block = block.reshape(rows * part, pairs, held * columns).transpose(1, 0, 2)
        if regrouped:
            block, regrouped[-1] = lax.optimization_barrier((block, regrouped[-1]))
        regrouped.append(lax.all_to_all(block, "pair", split_axis=0, concat_axis=0, tiled=True))
    every = [gathered(block, slabs, chunk) for chunk, block in enumerate(regrouped)]
    every[0], _, high, low = lax.optimization_barrier((every[0], regrouped[-1], high, low))
    outs = []
    for chunk in range(chunks):
        outs.append(run(every[chunk], high, low, sizes))
    for chunk in range(chunks):
        summed = lax.psum_scatter(outs[chunk], "pair", scatter_dimension=0, tiled=True)
        summed = summed.reshape(part, columns, integrals.shape[2], integrals.shape[3])
        outs[chunk] = summed.transpose(1, 0, 2, 3)
    return jnp.concatenate(outs, axis=1)


def solution(mesh):
    in_specs = (P("slab", None, None, "pair"), P("pair", None, "slab", None))
    out_specs = P("pair", None, "slab", None)
    return jax.shard_map(shards, mesh=mesh, in_specs=in_specs, out_specs=out_specs, check_vma=False)
```

```python
import functools

import jax
import jax.numpy as jnp
from jax import lax
from jax.experimental import pallas as pl
from jax.experimental.pallas import tpu as pltpu
from jax.sharding import PartitionSpec as P

PART = 2


def contract_kernel(sizes, *refs):
    slabs, pairs, rows, part, held, columns = sizes
    block_refs, (high_ref, low_ref, out_ref, rows_ref, left_ref) = refs[:slabs], refs[slabs:]
    me = lax.axis_index("slab")
    virtuals = slabs * rows
    wide = held * columns
    here = pl.program_id(0)
    tiles = rows_ref.shape[1]
    for code, block_ref in enumerate(block_refs):
        owner = pl.ds(pl.multiple_of((me ^ code) * (rows * part), 8), rows * part)
        for pair in range(pairs):
            for tile in range(tiles):
                lanes = min(128, wide - tile * 128)
                rows_ref[pair, tile, owner, pl.ds(0, lanes)] = block_ref[pair, :, pl.ds(tile * 128, lanes)]

    def picked(pair):
        window = pl.ds(here, virtuals, stride=part)
        return jnp.concatenate([rows_ref[pair, tile, window, :] for tile in range(tiles)], axis=1)[:, :wide]

    def mirrored(pair, carry):
        turned = jnp.transpose(picked(pair))
        target = pl.ds(pl.multiple_of(pair * columns, 8), columns)
        for k in range(held):
            for other in range(pairs):
                left_ref[target, pl.ds(other * wide + k * columns, columns)] = turned[
                    k * columns : (k + 1) * columns, other * columns : (other + 1) * columns
                ]
        return carry

    lax.fori_loop(0, pairs, mirrored, 0)
    for pair in range(pairs):
        window = pl.ds(pair * wide, wide)
        left_ref[:, window] = 2.0 * picked(pair) - left_ref[:, window]
    left = left_ref[...]
    left_high = left.astype(jnp.bfloat16)
    left_low = (left - left_high.astype(jnp.float32)).astype(jnp.bfloat16)
    dot = functools.partial(jnp.dot, preferred_element_type=jnp.float32)
    total = dot(left_high, high_ref[...]) + dot(left_high, low_ref[...]) + dot(left_low, high_ref[...])
    for pair in range(pairs):
        out_ref[pair, 0] = total[pair * columns : (pair + 1) * columns, :]


def contract(blocks, high, low, sizes):
    slabs, pairs, rows, part, held, columns = sizes
    virtuals = slabs * rows
    depth, width = high.shape
    whole = lambda shape: pl.BlockSpec(shape, lambda i: (0,) * len(shape), pipeline_mode=pl.Buffered(1))
    return pl.pallas_call(
        functools.partial(contract_kernel, sizes),
        grid=(part,),
        out_shape=jax.ShapeDtypeStruct((pairs, part, columns, width), jnp.float32),
        in_specs=[whole(block.shape) for block in blocks] + [whole(high.shape), whole(low.shape)],
        out_specs=pl.BlockSpec((pairs, 1, columns, width), lambda i: (0, i, 0, 0)),
        scratch_shapes=[
            pltpu.VMEM((pairs, pl.cdiv(held * columns, 128), virtuals * part, 128), jnp.float32),
            pltpu.VMEM((virtuals, depth), jnp.float32),
        ],
        compiler_params=pltpu.CompilerParams(vmem_limit_bytes=56 * 2**20),
        cost_estimate=pl.CostEstimate(
            flops=6 * virtuals * part * depth * width,
            bytes_accessed=4 * (virtuals * part * (depth + width) + depth * width),
            transcendentals=0,
        ),
    )(*blocks, high, low)


def contract_plain(blocks, high, low, sizes):
    slabs, pairs, rows, part, held, columns = sizes
    virtuals = slabs * rows
    order = lax.axis_index("slab") ^ jnp.arange(slabs)
    whole = jnp.stack(blocks)[order].reshape(slabs, pairs, rows, part, held, columns)
    whole = whole.transpose(3, 4, 0, 2, 1, 5).reshape(part, held, virtuals, virtuals)
    left = 2.0 * whole - jnp.swapaxes(whole, 2, 3)
    left = left.reshape(part, held, virtuals, pairs, columns).transpose(0, 2, 3, 1, 4)
    right = high.astype(jnp.float32) + low.astype(jnp.float32)
    total = jnp.dot(
        left.reshape(part * virtuals, -1), right,
        precision=lax.Precision.HIGH, preferred_element_type=jnp.float32,
    )
    return total.reshape(part, pairs, columns, -1).transpose(1, 0, 2, 3)


def gathered(block, slabs, turn):
    bits = [1 << n for n in range(1, slabs.bit_length() - 1)]
    turn = turn % max(len(bits), 1)
    blocks = {0: block}
    for bit in bits[turn:] + bits[:turn] + [1]:
        swaps = [(n, n ^ bit) for n in range(slabs)]
        for code in sorted(blocks):
            blocks[code ^ bit] = lax.ppermute(blocks[code], "slab", swaps)
    return [blocks[code] for code in range(slabs)]


def shards(amplitudes, integrals):
    pairs, slabs = lax.axis_size("pair"), lax.axis_size("slab")
    rows, batch, occupied, columns = amplitudes.shape
    held = occupied // pairs
    part = PART if batch % PART == 0 else 1
    chunks = batch // part
    sizes = (slabs, pairs, rows, part, held, columns)
    run = contract if columns % 8 == 0 and (rows * part) % 8 == 0 else contract_plain
    right = integrals.reshape(held, pairs, columns, -1).transpose(1, 0, 2, 3)
    right = right.reshape(held * pairs * columns, -1)
    rounded = lax.reduce_precision(right, 8, 7)
    high = rounded.astype(jnp.bfloat16)
    low = (right - rounded).astype(jnp.bfloat16)
    regrouped = []
    for chunk in range(chunks):
        block = lax.slice_in_dim(amplitudes, chunk * part, (chunk + 1) * part, axis=1)
        block = block.reshape(rows * part, pairs, held * columns).transpose(1, 0, 2)
        if regrouped:
            block, regrouped[-1] = lax.optimization_barrier((block, regrouped[-1]))
        regrouped.append(lax.all_to_all(block, "pair", split_axis=0, concat_axis=0, tiled=True))
    ahead = 2 if run is contract and chunks > 2 else 1
    every = [gathered(block, slabs, chunk) for chunk, block in enumerate(regrouped[:ahead])]
    every, regrouped[-1], high, low = lax.optimization_barrier((every, regrouped[-1], high, low))
    outs = []
    for chunk in range(chunks):
        if chunk >= ahead:
            if ahead > 1 and chunk == ahead:
                regrouped[chunk], outs[-1] = lax.optimization_barrier((regrouped[chunk], outs[-1]))
            every.append(gathered(regrouped[chunk], slabs, chunk))
        outs.append(run(every[chunk], high, low, sizes))
    for chunk in range(chunks):
        summed = lax.psum_scatter(outs[chunk], "pair", scatter_dimension=0, tiled=True)
        summed = summed.reshape(part, columns, integrals.shape[2], integrals.shape[3])
        outs[chunk] = summed.transpose(1, 0, 2, 3)
    return jnp.concatenate(outs, axis=1)


def solution(mesh):
    in_specs = (P("slab", None, None, "pair"), P("pair", None, "slab", None))
    out_specs = P("pair", None, "slab", None)
    return jax.shard_map(shards, mesh=mesh, in_specs=in_specs, out_specs=out_specs, check_vma=False)
```
